32 devices in a mesh: dp: 8 (over z, x), seq: 4 (over y, core).
Axes of the slice: x: 2, y: 2, z: 4, core: 2. Of those that a mesh axis runs over, the one named last changes fastest.
Arguments:
- spatial_qkv: bfloat16 [8, 3, 4, 128, 1152], P('dp', None, 'seq'), may hold values from -24 to 24
- temporal_qkv: bfloat16 [8, 3, 4, 128, 1152], P('dp', None, 'seq'), may hold values from -24 to 24
- cotangent: bfloat16 [8, 4, 128, 1152], P('dp', 'seq'), may hold values from -6 to 6
- spatial_gate: float32 [8, 1152], P('dp'), may hold values from -4 to 4
- temporal_gate: float32 [8, 1152], P('dp'), may hold values from -4 to 4
- temporal_proj: bfloat16 [1152, 1152], replicated, may hold values from -0.1875 to 0.1875
- live_counts: int32 [8, 2], P('dp'), may hold values from 2 to 128, as said below
Outputs:
- temporal_qkv_grad: bfloat16 [8, 3, 4, 128, 1152], P('dp', None, 'seq')
- spatial_proj_grad: float32 [1152, 1152], P('seq', 'dp')
- temporal_proj_grad: float32 [1152, 1152], P('seq', 'dp')
The draws below stay inside these ranges and needn't reach their ends.
Inputs may be any that keep to these rules, and one draw needn't show every extreme that they name: live_counts[g, 0] counts a clip's live frames, at most 4; live_counts[g, 1] counts the live positions of each of its frames, at most 128; in every draw some clip has all 4 frames and all 128 positions live.
All inputs are finite; a program needn't handle non-finite values.
Results may differ from the reference program's by a relative error of at most 0.015.
Values may be sent and summed in bfloat16 or wider, within the bound.
A program may use at most 64 MiB of HBM per device.

```python
import jax
import jax.numpy as jnp
from jax import lax

D = 1152
HEADS = 16
FR_DEV = 1
POS = 128
HD = 72
FRAMES = 4
GROUPS = 8
N_SEQ = 4


def make_attention_inputs(base_key):
    first_key = jax.random.fold_in(base_key, 0)
    drawn = jax.random.truncated_normal(first_key, -6.0, 6.0, (GROUPS, 3, FRAMES, POS, D), jnp.float32)
    return drawn.astype(jnp.bfloat16)


def draw_spatial_qkv(key, part):
    return make_attention_inputs(jax.random.fold_in(key, 11))


def draw_temporal_qkv(key, part):
    return make_attention_inputs(jax.random.fold_in(key, 12))


def draw_live_counts(key, part):
    first_key, second_key, third_key = jax.random.split(jax.random.fold_in(key, 13), 3)
    frame_counts = jax.random.randint(first_key, (GROUPS,), max(2, FRAMES // 4), FRAMES + 1)
    position_counts = jax.random.randint(second_key, (GROUPS,), max(2, POS // 4), POS + 1)
    full_group = jax.random.randint(third_key, (), 0, GROUPS)
    group_ids = jnp.arange(GROUPS)
    frame_counts = jnp.where(group_ids == full_group, FRAMES, frame_counts)
    position_counts = jnp.where(group_ids == full_group, POS, position_counts)
    return jnp.stack([frame_counts, position_counts], axis=1).astype(jnp.int32)


def level_of(stream_key, dims, pieces, low, high):
    factor_of = 1.0
    for dim, blocks in pieces:
        steps = jax.random.uniform(jax.random.fold_in(jax.random.fold_in(stream_key, 6), dim), (blocks,), jnp.float32, low / len(pieces), high / len(pieces))
        factor_of = factor_of * jnp.repeat(jnp.exp(steps), dims[dim] // blocks).reshape((-1,) + (1,) * (len(dims) - 1 - dim))
    return factor_of


def normal_values(own_key, shape, width, most, cuts=(), kind=jnp.bfloat16):
    gain = level_of(own_key, shape, cuts, -0.22, 0.18) if cuts else 1.0
    array = jax.random.normal(own_key, shape, jnp.float32) * width * gain
    return jnp.minimum(jnp.maximum(array, -most), most).astype(kind)


def setup_inputs(seed: int = 0) -> dict:
    splits = jax.random.split(jax.random.key(seed), 8)
    spatial_qkv = draw_spatial_qkv(jax.random.fold_in(splits[7], 71), 0)
    temporal_qkv = draw_temporal_qkv(jax.random.fold_in(splits[7], 71), 0)
    cotangent = normal_values(splits[2], (GROUPS, FRAMES, POS, D), 1.0, 6.0, ((0, 8), (1, 4)))
    spatial_gate = normal_values(splits[3], (GROUPS, D), 1.0, 4.0, ((0, 8),), jnp.float32)
    temporal_gate = normal_values(splits[4], (GROUPS, D), 1.0, 4.0, ((0, 8),), jnp.float32)
    temporal_proj = normal_values(splits[5], (D, D), D ** -0.5, 0.1875)
    live_counts = draw_live_counts(jax.random.fold_in(splits[7], 71), 0)
    return {"spatial_qkv": spatial_qkv, "temporal_qkv": temporal_qkv, "cotangent": cotangent, "spatial_gate": spatial_gate, "temporal_gate": temporal_gate, "temporal_proj": temporal_proj, "live_counts": live_counts}


def attend(queries, key_block, value_block, key_keep, score_form, mix_form):
    head_split = queries.shape[:-1] + (HEADS, HD)
    q_heads = queries.astype(jnp.float32).reshape(head_split)
    k_heads = key_block.astype(jnp.float32).reshape(head_split)
    v_heads = value_block.astype(jnp.float32).reshape(head_split)
    scores = jnp.einsum(score_form, q_heads, k_heads) * HD ** (-0.5)
    scores = jnp.where(key_keep[:, None, None, :], scores, -1e+30)
    shifted = scores - lax.optimization_barrier(jnp.max(scores, axis=-1, keepdims=True))
    expo = jnp.exp(shifted)
    attention_weights = expo / lax.optimization_barrier(jnp.sum(expo, axis=-1, keepdims=True))
    rounded = lax.optimization_barrier(attention_weights.astype(jnp.bfloat16)).astype(jnp.float32)
    mixed = jnp.einsum(mix_form, rounded, v_heads)
    return mixed.reshape(queries.shape)

def block_parts(outputs, errors):
    left = outputs.reshape(N_SEQ, FR_DEV * POS, D).astype(jnp.float32)
    right = errors.reshape(N_SEQ, FR_DEV * POS, D).astype(jnp.float32)
    parts = jnp.einsum('btr,btc->brc', left, right)
    parts = lax.optimization_barrier(parts.astype(jnp.bfloat16)).astype(jnp.float32)
    return lax.optimization_barrier(jnp.sum(parts, axis=0))

def reference(spatial_qkv, temporal_qkv, cotangent, spatial_gate, temporal_gate, temporal_proj, live_counts):

    def one_group(accumulated, group_items):
        s_qkv, t_qkv, incoming, s_gate, t_gate, counts = group_items
        frame_ids = jnp.arange(FRAMES, dtype=jnp.int32)
        position_ids = jnp.arange(POS, dtype=jnp.int32)
        token_mask = ((frame_ids[:, None] < counts[0]) & (position_ids[None, :] < counts[1])).astype(jnp.float32)
        flowing = token_mask[:, :, None] * incoming.astype(jnp.float32)
        spatial_error = (flowing * s_gate).astype(jnp.bfloat16)
        temporal_error = (flowing * t_gate).astype(jnp.bfloat16)
        temporal_back = jnp.dot(temporal_error.reshape(FRAMES * POS, D), temporal_proj.T, preferred_element_type=jnp.float32).astype(jnp.bfloat16).reshape(FRAMES, POS, D)
        spatial_keep = jnp.broadcast_to(position_ids[None, :] < counts[1], (FRAMES, POS))
        spatial_out = attend(s_qkv[0], s_qkv[1], s_qkv[2], spatial_keep, 'bqhd,bkhd->bhqk', 'bhqk,bkhd->bqhd').astype(jnp.bfloat16)
        temporal_keep = jnp.broadcast_to(frame_ids[None, :] < counts[0], (POS, FRAMES))

        def temporal_attend(queries, key_block, value_block):
            return attend(queries, key_block, value_block, temporal_keep, 'qbhd,kbhd->bhqk', 'bhqk,kbhd->qbhd')
        temporal_result, pullback = jax.vjp(temporal_attend, t_qkv[0], t_qkv[1], t_qkv[2])
        temporal_out = temporal_result.astype(jnp.bfloat16)
        input_grads = jnp.stack(pullback(temporal_back.astype(jnp.float32)))
        spatial_sum = accumulated[0] + block_parts(spatial_out, spatial_error)
        temporal_sum = accumulated[1] + block_parts(temporal_out, temporal_error)
        return ((spatial_sum, temporal_sum), input_grads)
    start = (jnp.zeros((D, D), jnp.float32), jnp.zeros((D, D), jnp.float32))
    sums, all_grads = lax.scan(one_group, start, (spatial_qkv, temporal_qkv, cotangent, spatial_gate, temporal_gate, live_counts))
    return (all_grads, sums[0], sums[1])
```

```python
import functools

import jax
import jax.numpy as jnp
from jax import lax
from jax.experimental import pallas as pl
from jax.experimental.pallas import tpu as pltpu
from jax.sharding import PartitionSpec as P

HEADS = 16
HD = 72
MESH = pl.DeviceIdType.MESH
F32 = jnp.float32
BF16 = jnp.bfloat16


def attend(queries, key_block, value_block, key_keep, score_form, mix_form):
    head_split = queries.shape[:-1] + (HEADS, HD)
    q_heads = queries.reshape(head_split)
    k_heads = key_block.reshape(head_split)
    v_heads = value_block.reshape(head_split)
    scores = jnp.einsum(score_form, q_heads, k_heads, preferred_element_type=jnp.float32) * HD ** (
        -0.5
    )
    scores = jnp.where(key_keep[:, None, None, :], scores, -1e30)
    shifted = scores - jnp.max(scores, axis=-1, keepdims=True)
    expo = jnp.exp(shifted)
    attention_weights = (expo / jnp.sum(expo, axis=-1, keepdims=True)).astype(jnp.bfloat16)
    mixed = jnp.einsum(mix_form, attention_weights, v_heads, preferred_element_type=jnp.float32)
    return mixed.reshape(queries.shape)


def body(
    spatial_qkv, temporal_qkv, cotangent, spatial_gate, temporal_gate, temporal_proj, live_counts
):
    spatial = spatial_qkv[0]
    temporal = temporal_qkv[0]
    incoming = cotangent[0]
    frame_count, position_count, width = incoming.shape
    group_size = lax.axis_size("seq")
    member = lax.axis_index("seq")
    live_frames = live_counts[0, 0]
    live_positions = live_counts[0, 1]
    frame_ids = member * frame_count + jnp.arange(frame_count, dtype=jnp.int32)
    position_ids = jnp.arange(position_count, dtype=jnp.int32)
    token_mask = (
        (frame_ids[:, None] < live_frames) & (position_ids[None, :] < live_positions)
    ).astype(jnp.float32)
    flowing = token_mask[:, :, None] * incoming.astype(jnp.float32)
    temporal_error = (flowing * temporal_gate[0]).astype(jnp.bfloat16)
    temporal_back = lax.dot_general(
        temporal_error, temporal_proj, (((2,), (1,)), ((), ())), preferred_element_type=jnp.float32
    ).astype(jnp.bfloat16)
    stacked = jnp.concatenate([temporal, temporal_back[None]], axis=0)
    exchanged = lax.all_to_all(stacked, "seq", split_axis=2, concat_axis=1, tiled=True)
    spatial_keep = position_ids[None, :] < live_positions
    spatial_out = attend(
        spatial[0], spatial[1], spatial[2], spatial_keep, "bqhd,bkhd->bhqk", "bhqk,bkhd->bqhd"
    ).astype(jnp.bfloat16)
    total_frames = exchanged.shape[1]
    slice_positions = exchanged.shape[2]
    temporal_keep = jnp.broadcast_to(
        jnp.arange(total_frames, dtype=jnp.int32)[None, :] < live_frames,
        (slice_positions, total_frames),
    )

    def temporal_attend(queries, key_block, value_block):
        return attend(
            queries, key_block, value_block, temporal_keep, "qbhd,kbhd->bhqk", "bhqk,kbhd->qbhd"
        )

    temporal_result, pullback = jax.vjp(temporal_attend, exchanged[0], exchanged[1], exchanged[2])
    temporal_out = temporal_result.astype(jnp.bfloat16)
    input_grads = jnp.stack(pullback(exchanged[3].astype(jnp.float32)))
    temporal_frames = lax.all_to_all(temporal_out, "seq", split_axis=0, concat_axis=1, tiled=True)
    grads_home = lax.all_to_all(input_grads, "seq", split_axis=1, concat_axis=2, tiled=True)
    tokens = frame_count * position_count
    flat_spatial = spatial_out.reshape(tokens, width)
    flat_temporal = temporal_frames.reshape(tokens, width)
    slice_width = width // group_size
    column_spatial, column_temporal = (
        lax.all_to_all(flat_spatial, "seq", split_axis=1, concat_axis=0, tiled=True),
        lax.all_to_all(flat_temporal, "seq", split_axis=1, concat_axis=0, tiled=True),
    )
    spatial_scale = spatial_gate[0]
    temporal_scale = temporal_gate[0]
    starting = jnp.zeros((slice_width, 2, width), jnp.float32)
    cot_piece = lax.all_gather(incoming.reshape(tokens, width), "seq", axis=0, tiled=True)
    shards = cot_piece.shape[0] // tokens

    def one_block(block, total):
        offset = (block * tokens).astype(jnp.int32)
        rows = lax.dynamic_slice_in_dim(cot_piece, offset, tokens, 0)
        token_index = offset + jnp.arange(tokens, dtype=jnp.int32)
        frame_of = token_index // position_count
        position_of = token_index % position_count
        row_keep = ((frame_of < live_frames) & (position_of < live_positions)).astype(jnp.float32)
        masked_rows = row_keep[:, None] * rows.astype(jnp.float32)
        error_first = (masked_rows * spatial_scale).astype(jnp.bfloat16)
        error_second = (masked_rows * temporal_scale).astype(jnp.bfloat16)
        cols_first = lax.dynamic_slice_in_dim(column_spatial, offset, tokens, 0)
        cols_second = lax.dynamic_slice_in_dim(column_temporal, offset, tokens, 0)
        part_first = lax.dot_general(
            cols_first, error_first, (((0,), (0,)), ((), ())), preferred_element_type=jnp.float32
        )
        part_second = lax.dot_general(
            cols_second, error_second, (((0,), (0,)), ((), ())), preferred_element_type=jnp.float32
        )
        part_first = part_first.astype(jnp.bfloat16).astype(jnp.float32)
        part_second = part_second.astype(jnp.bfloat16).astype(jnp.float32)
        return total + jnp.stack([part_first, part_second], axis=1)

    partial_sum = lax.fori_loop(0, shards, one_block, starting)
    summed = lax.psum_scatter(partial_sum, "dp", scatter_dimension=2, tiled=True)
    return (grads_home[None], summed[:, 0], summed[:, 1])


def kernel(
    n, nb, counts, sgate, tgate, sqkv_hbm, tqkv_hbm, cot_hbm, proj_hbm,
    g_out, sp_out, tp_out,
    sqkv, tqkv, cot, proj, cot_t, q_t, v_t, o_t, so, so_r, tq, tq_r, tqf, gf,
    err, err2, ot, do_t, part, xr, zs, zr, gs, gr,
    loc_sem, cs, cr, fs, fr, ss, sr, ts, tr, us, ur, xss, xrs, zss, zrs,
):
    me = lax.axis_index("seq")
    dp = lax.axis_index("dp")
    pos, width = cot.shape
    sl = width // n
    rows = width // nb
    ny, outer = n // 2, nb // 2
    y, c = me // 2, me % 2
    mate = y * 2 + 1 - c
    oz, ox = dp // 2, dp % 2
    scale = HD ** (-0.5)

    loads = [
        pltpu.make_async_copy(cot_hbm, cot, loc_sem.at[0]),
        pltpu.make_async_copy(sqkv_hbm, sqkv, loc_sem.at[1]),
        pltpu.make_async_copy(tqkv_hbm, tqkv, loc_sem.at[2]),
        pltpu.make_async_copy(proj_hbm.at[me], proj, loc_sem.at[3]),
    ]
    for load in loads:
        load.start()
    barrier = pltpu.get_barrier_semaphore()
    for j in range(1, n):
        pl.semaphore_signal(barrier, inc=1, device_id=(dp, (me + j) % n), device_id_type=MESH)
    pl.semaphore_signal(barrier, inc=1, device_id=(oz * 2 + 1 - ox, me), device_id_type=MESH)
    for j in range(1, outer):
        pl.semaphore_signal(
            barrier, inc=1, device_id=((oz + j) % outer * 2 + ox, me), device_id_type=MESH
        )

    def remote(src, dst, s_sem, r_sem, to):
        return pltpu.make_async_remote_copy(
            src_ref=src, dst_ref=dst, send_sem=s_sem, recv_sem=r_sem, device_id=to,
            device_id_type=MESH,
        )

    def turned(value):
        return value.astype(F32).T

    loads[0].wait()
    cot_t[me] = turned(cot[...]).astype(BF16)
    pl.semaphore_wait(barrier, (n - 1) + 1 + (outer - 1))

    sent = []

    def send(copy):
        copy.start()
        sent.append(copy)

    def y_copy(j):
        return remote(
            cot_t.at[me], cot_t.at[me], cs.at[j - 1], cr.at[j - 1], (dp, (y + j) % ny * 2 + c)
        )

    def pass_copy(j, core):
        slot = (y + ny - j) % ny * 2 + core
        return remote(cot_t.at[slot], cot_t.at[slot], fs.at[j], fr.at[j], (dp, mate))

    for j in range(1, ny):
        send(y_copy(j))
    send(pass_copy(0, c))

    live_frames = counts[0, 0]
    live_positions = counts[0, 1]

    loads[1].wait()
    q_t[...] = turned(sqkv[0])
    v_t[...] = turned(sqkv[2])
    key_keep = lax.broadcasted_iota(jnp.int32, (pos, pos), 0) < live_positions
    for h in range(HEADS):
        low = h * HD
        w0 = low // 128 * 128
        w1 = -(-(low + HD) // 128) * 128
        row = lax.broadcasted_iota(jnp.int32, (w1 - w0, pos), 0)
        inside = (row >= low - w0) & (row < low - w0 + HD)
        q_win = jnp.where(inside, q_t[w0:w1, :], 0.0).astype(BF16)
        scores = jnp.dot(sqkv[1, :, w0:w1], q_win, preferred_element_type=F32) * scale
        scores = jnp.where(key_keep, scores, -1e30)
        expo = jnp.exp(scores - jnp.max(scores, axis=0, keepdims=True))
        weights = (expo / jnp.sum(expo, axis=0, keepdims=True)).astype(BF16)
        o_t[low : low + HD, :] = jnp.dot(
            v_t[low : low + HD, :].astype(BF16), weights, preferred_element_type=F32
        )
    for s in range(n):
        so[s] = o_t[s * sl : (s + 1) * sl, :].astype(BF16)
    so_r[me] = so[me]

    def swap(src, dst, s_sem, r_sem, j):
        to = (me + j) % n
        return remote(src.at[to], dst.at[me], s_sem.at[j - 1], r_sem.at[j - 1], (dp, to))

    def arrive(src, dst, s_sem, r_sem):
        for j in range(1, n):
            origin = (me + n - j) % n
            remote(
                src.at[origin], dst.at[origin], s_sem.at[j - 1], r_sem.at[j - 1], (dp, origin)
            ).wait_recv()

    for j in range(1, n):
        send(swap(so, so_r, ss, sr, j))

    loads[2].wait()
    for m in range(3):
        flat = turned(tqkv[m]).astype(BF16)
        for s in range(n):
            tq[s, m] = flat[s * sl : (s + 1) * sl, :]
    tq_r[me] = tq[me]
    for j in range(1, n):
        send(swap(tq, tq_r, ts, tr, j))

    def gate_rows(gate):
        return jnp.broadcast_to(gate[...], (pos, width)).T

    for j in range(1, ny):
        slot = (y + ny - j) % ny * 2 + c
        remote(
            cot_t.at[slot], cot_t.at[slot], cs.at[j - 1], cr.at[j - 1], (dp, mate)
        ).wait_recv()
        send(pass_copy(j, c))
    for j in range(ny):
        pass_copy(j, 1 - c).wait_recv()

    lane = lax.broadcasted_iota(jnp.int32, (1, pos), 1)
    keep = [
        ((lane < live_positions) & (f < live_frames)).astype(F32) for f in range(n)
    ]

    def errors(target, gate):
        columns = gate_rows(gate)
        for f in range(n):
            target[:, f * pos : (f + 1) * pos] = (
                keep[f] * cot_t[f].astype(F32) * columns
            ).astype(BF16)

    def product(p, source, outs):
        for d in range(nb):
            part[p, d] = lax.dot_general(
                source[d * rows : (d + 1) * rows, :], outs, (((1,), (1,)), ((), ())),
                preferred_element_type=F32,
            ).astype(BF16)

    def pair_copy(p, j):
        z = (oz + j) % outer
        return remote(
            part.at[p, z * 2 + 1 - ox], xr.at[p, j], xss.at[p, j], xrs.at[p, j],
            (oz * 2 + 1 - ox, me),
        )

    def line_copy(p, j):
        z = (oz + j) % outer
        return remote(
            zs.at[p, j - 1], zr.at[p, j - 1], zss.at[p, j - 1], zrs.at[p, j - 1], (z * 2 + ox, me)
        )

    order = list(range(1, outer)) + [0]

    def pair_start(p):
        for j in order:
            send(pair_copy(p, j))

    def line_start(p):
        for j in order:
            z = (oz + j) % outer
            pair_copy(p, j).wait_recv()
            if j:
                zs[p, j - 1] = (
                    part[p, z * 2 + ox].astype(F32) + xr[p, j].astype(F32)
                ).astype(BF16)
                send(line_copy(p, j))

    def line_end(p, out):
        total = part[p, oz * 2 + ox].astype(F32) + xr[p, 0].astype(F32)
        for j in range(1, outer):
            line_copy(p, j).wait_recv()
            total = total + zr[p, j - 1].astype(F32)
        out[...] = total

    errors(err, sgate)
    arrive(so, so_r, ss, sr)
    product(0, err, jnp.concatenate([so_r[f] for f in range(n)], axis=1))
    pair_start(0)

    errors(err2, tgate)
    loads[3].wait()
    do_t[...] = (
        jnp.dot(proj[...], err2[...], preferred_element_type=F32).astype(BF16).astype(F32)
    )
    line_start(0)

    arrive(tq, tq_r, ts, tr)
    for f in range(n):
        for m in range(3):
            tqf[f, m] = tq_r[f, m].astype(F32)
    kept = []
    for h in range(sl // HD):
        band = slice(h * HD, (h + 1) * HD)
        ks = [tqf[g, 1, band, :] for g in range(n)]
        vs = [tqf[g, 2, band, :] for g in range(n)]
        for f in range(n):
            q = tqf[f, 0, band, :]
            row = [
                jnp.where(g < live_frames, jnp.sum(q * ks[g], axis=0, keepdims=True) * scale, -1e30)
                for g in range(n)
            ]
            top = functools.reduce(jnp.maximum, row)
            expo = [jnp.exp(value - top) for value in row]
            total = functools.reduce(jnp.add, expo)
            soft = [value / total for value in expo]
            rounded = [value.astype(BF16).astype(F32) for value in soft]
            kept.append((soft, rounded))
            ot[band, f * pos : (f + 1) * pos] = functools.reduce(
                jnp.add, [rounded[g] * vs[g] for g in range(n)]
            )
    product(1, err2, ot[...].astype(BF16))
    pair_start(1)

    for h in range(sl // HD):
        band = slice(h * HD, (h + 1) * HD)
        slopes = []
        for f in range(n):
            soft, rounded = kept[h * n + f]
            back = do_t[band, f * pos : (f + 1) * pos]
            dw = [
                jnp.sum(back * tqf[g, 2, band, :], axis=0, keepdims=True).astype(BF16).astype(F32)
                for g in range(n)
            ]
            mean = functools.reduce(jnp.add, [soft[g] * dw[g] for g in range(n)])
            slopes.append([soft[g] * (dw[g] - mean) * scale for g in range(n)])
        for f in range(n):
            gf[f, 0, band, :] = functools.reduce(
                jnp.add, [slopes[f][g] * tqf[g, 1, band, :] for g in range(n)]
            )
            gf[f, 1, band, :] = functools.reduce(
                jnp.add, [slopes[g][f] * tqf[g, 0, band, :] for g in range(n)]
            )
            gf[f, 2, band, :] = functools.reduce(
                jnp.add,
                [
                    kept[h * n + g][1][f] * do_t[band, g * pos : (g + 1) * pos]
                    for g in range(n)
                ],
            )
    for f in range(n):
        for m in range(3):
            gs[f, m] = gf[f, m].astype(BF16)
    gr[me] = gs[me]
    for j in range(1, n):
        send(swap(gs, gr, us, ur, j))

    line_end(0, sp_out)
    line_start(1)
    arrive(gs, gr, us, ur)
    for s in range(n):
        for m in range(3):
            g_out[m, s * sl : (s + 1) * sl, :] = gr[s, m]
    line_end(1, tp_out)
    for copy in sent:
        copy.wait_send()


def kernel_body(
    n, nb, spatial_qkv, temporal_qkv, cotangent, spatial_gate, temporal_gate, temporal_proj, live_counts
):
    pos, width = cotangent.shape[2:]
    sl, rows, outer, ny = width // n, width // nb, nb // 2, n // 2
    vm, dma = pltpu.VMEM, pltpu.SemaphoreType.DMA
    whole = pl.BlockSpec(memory_space=pltpu.VMEM)
    left = pl.BlockSpec(memory_space=pl.ANY)
    grads, first, second = pl.pallas_call(
        functools.partial(kernel, n, nb),
        out_shape=(
            jax.ShapeDtypeStruct((3, width, pos), BF16),
            jax.ShapeDtypeStruct((rows, sl), F32),
            jax.ShapeDtypeStruct((rows, sl), F32),
        ),
        in_specs=[pl.BlockSpec(memory_space=pltpu.SMEM), whole, whole, left, left, left, left],
        out_specs=(whole, whole, whole),
        scratch_shapes=[
            vm((3, pos, width), BF16), vm((3, pos, width), BF16), vm((pos, width), BF16),
            vm((sl, width), BF16), vm((n, width, pos), BF16),
            vm((width, pos), F32), vm((width, pos), F32), vm((width, pos), F32),
            vm((n, sl, pos), BF16), vm((n, sl, pos), BF16),
            vm((n, 3, sl, pos), BF16), vm((n, 3, sl, pos), BF16),
            vm((n, 3, sl, pos), F32), vm((n, 3, sl, pos), F32),
            vm((width, n * pos), BF16), vm((width, n * pos), BF16),
            vm((sl, n * pos), F32), vm((sl, n * pos), F32),
            vm((2, nb, rows, sl), BF16), vm((2, outer, rows, sl), BF16),
            vm((2, outer - 1, rows, sl), BF16), vm((2, outer - 1, rows, sl), BF16),
            vm((n, 3, sl, pos), BF16), vm((n, 3, sl, pos), BF16),
            dma((4,)), dma((ny - 1,)), dma((ny - 1,)), dma((ny,)), dma((ny,)),
            dma((n - 1,)), dma((n - 1,)), dma((n - 1,)), dma((n - 1,)), dma((n - 1,)), dma((n - 1,)),
            dma((2, outer)), dma((2, outer)), dma((2, outer - 1)), dma((2, outer - 1)),
        ],
        compiler_params=pltpu.CompilerParams(
            collective_id=0, has_side_effects=True, vmem_limit_bytes=56 * 1024 * 1024
        ),
    )(
        live_counts, spatial_gate, temporal_gate,
        spatial_qkv.reshape(3, pos, width), temporal_qkv.reshape(3, pos, width),
        cotangent.reshape(pos, width), temporal_proj.reshape(n, sl, width),
    )
    grads = grads.transpose(0, 2, 1)[None, :, None]
    return grads, first.T, second.T


def solution(mesh):
    n, nb = mesh.shape["seq"], mesh.shape["dp"]

    def chosen(*args):
        cot = args[2]
        _, frames, pos, width = cot.shape
        fits = frames == 1 and pos == 128 and width == HEADS * HD and n % 2 == 0 and nb % 2 == 0
        fits = fits and n > 2 and nb > 2 and HEADS % n == 0
        if fits and width // n % 16 == 0 and width // nb % 16 == 0:
            return kernel_body(n, nb, *args)
        return body(*args)

    return jax.shard_map(
        chosen,
        mesh=mesh,
        in_specs=(
            P("dp", None, "seq", None, None),
            P("dp", None, "seq", None, None),
            P("dp", "seq", None, None),
            P("dp", None),
            P("dp", None),
            P(),
            P("dp", None),
        ),
        out_specs=(P("dp", None, "seq", None, None), P("seq", "dp"), P("seq", "dp")),
        check_vma=False,
    )
```

```python
import functools

import jax
import jax.numpy as jnp
from jax import lax
from jax.experimental import pallas as pl
from jax.experimental.pallas import tpu as pltpu
from jax.sharding import PartitionSpec as P

HEADS = 16
HD = 72
MESH = pl.DeviceIdType.MESH
F32 = jnp.float32
BF16 = jnp.bfloat16


def attend(queries, key_block, value_block, key_keep, score_form, mix_form):
    head_split = queries.shape[:-1] + (HEADS, HD)
    q_heads = queries.reshape(head_split)
    k_heads = key_block.reshape(head_split)
    v_heads = value_block.reshape(head_split)
    scores = jnp.einsum(score_form, q_heads, k_heads, preferred_element_type=jnp.float32) * HD ** (
        -0.5
    )
    scores = jnp.where(key_keep[:, None, None, :], scores, -1e30)
    shifted = scores - jnp.max(scores, axis=-1, keepdims=True)
    expo = jnp.exp(shifted)
    attention_weights = (expo / jnp.sum(expo, axis=-1, keepdims=True)).astype(jnp.bfloat16)
    mixed = jnp.einsum(mix_form, attention_weights, v_heads, preferred_element_type=jnp.float32)
    return mixed.reshape(queries.shape)


def body(
    spatial_qkv, temporal_qkv, cotangent, spatial_gate, temporal_gate, temporal_proj, live_counts
):
    spatial = spatial_qkv[0]
    temporal = temporal_qkv[0]
    incoming = cotangent[0]
    frame_count, position_count, width = incoming.shape
    group_size = lax.axis_size("seq")
    member = lax.axis_index("seq")
    live_frames = live_counts[0, 0]
    live_positions = live_counts[0, 1]
    frame_ids = member * frame_count + jnp.arange(frame_count, dtype=jnp.int32)
    position_ids = jnp.arange(position_count, dtype=jnp.int32)
    token_mask = (
        (frame_ids[:, None] < live_frames) & (position_ids[None, :] < live_positions)
    ).astype(jnp.float32)
    flowing = token_mask[:, :, None] * incoming.astype(jnp.float32)
    temporal_error = (flowing * temporal_gate[0]).astype(jnp.bfloat16)
    temporal_back = lax.dot_general(
        temporal_error, temporal_proj, (((2,), (1,)), ((), ())), preferred_element_type=jnp.float32
    ).astype(jnp.bfloat16)
    stacked = jnp.concatenate([temporal, temporal_back[None]], axis=0)
    exchanged = lax.all_to_all(stacked, "seq", split_axis=2, concat_axis=1, tiled=True)
    spatial_keep = position_ids[None, :] < live_positions
    spatial_out = attend(
        spatial[0], spatial[1], spatial[2], spatial_keep, "bqhd,bkhd->bhqk", "bhqk,bkhd->bqhd"
    ).astype(jnp.bfloat16)
    total_frames = exchanged.shape[1]
    slice_positions = exchanged.shape[2]
    temporal_keep = jnp.broadcast_to(
        jnp.arange(total_frames, dtype=jnp.int32)[None, :] < live_frames,
        (slice_positions, total_frames),
    )

    def temporal_attend(queries, key_block, value_block):
        return attend(
            queries, key_block, value_block, temporal_keep, "qbhd,kbhd->bhqk", "bhqk,kbhd->qbhd"
        )

    temporal_result, pullback = jax.vjp(temporal_attend, exchanged[0], exchanged[1], exchanged[2])
    temporal_out = temporal_result.astype(jnp.bfloat16)
    input_grads = jnp.stack(pullback(exchanged[3].astype(jnp.float32)))
    temporal_frames = lax.all_to_all(temporal_out, "seq", split_axis=0, concat_axis=1, tiled=True)
    grads_home = lax.all_to_all(input_grads, "seq", split_axis=1, concat_axis=2, tiled=True)
    tokens = frame_count * position_count
    flat_spatial = spatial_out.reshape(tokens, width)
    flat_temporal = temporal_frames.reshape(tokens, width)
    slice_width = width // group_size
    column_spatial, column_temporal = (
        lax.all_to_all(flat_spatial, "seq", split_axis=1, concat_axis=0, tiled=True),
        lax.all_to_all(flat_temporal, "seq", split_axis=1, concat_axis=0, tiled=True),
    )
    spatial_scale = spatial_gate[0]
    temporal_scale = temporal_gate[0]
    starting = jnp.zeros((slice_width, 2, width), jnp.float32)
    cot_piece = lax.all_gather(incoming.reshape(tokens, width), "seq", axis=0, tiled=True)
    shards = cot_piece.shape[0] // tokens

    def one_block(block, total):
        offset = (block * tokens).astype(jnp.int32)
        rows = lax.dynamic_slice_in_dim(cot_piece, offset, tokens, 0)
        token_index = offset + jnp.arange(tokens, dtype=jnp.int32)
        frame_of = token_index // position_count
        position_of = token_index % position_count
        row_keep = ((frame_of < live_frames) & (position_of < live_positions)).astype(jnp.float32)
        masked_rows = row_keep[:, None] * rows.astype(jnp.float32)
        error_first = (masked_rows * spatial_scale).astype(jnp.bfloat16)
        error_second = (masked_rows * temporal_scale).astype(jnp.bfloat16)
        cols_first = lax.dynamic_slice_in_dim(column_spatial, offset, tokens, 0)
        cols_second = lax.dynamic_slice_in_dim(column_temporal, offset, tokens, 0)
        part_first = lax.dot_general(
            cols_first, error_first, (((0,), (0,)), ((), ())), preferred_element_type=jnp.float32
        )
        part_second = lax.dot_general(
            cols_second, error_second, (((0,), (0,)), ((), ())), preferred_element_type=jnp.float32
        )
        part_first = part_first.astype(jnp.bfloat16).astype(jnp.float32)
        part_second = part_second.astype(jnp.bfloat16).astype(jnp.float32)
        return total + jnp.stack([part_first, part_second], axis=1)

    partial_sum = lax.fori_loop(0, shards, one_block, starting)
    summed = lax.psum_scatter(partial_sum, "dp", scatter_dimension=2, tiled=True)
    return (grads_home[None], summed[:, 0], summed[:, 1])


def kernel(
    n, nb, groups, counts, sgate, tgate, sqkv_hbm, tqkv_hbm, cot_hbm, proj_hbm,
    g_out, sum_out,
    sqkv, tqkv, cot, proj, cot_t, q_t, v_t, o_t, so, so_r, tq, tq_r, tqf, gf,
    err, err2, ot, do_t, part, xr, zs, zr, gs, gr,
    loc_sem, cs, cr, fs, fr, ss, sr, ts, tr, us, ur, xss, xrs, zss, zrs,
):
    me = lax.axis_index("seq")
    dp = lax.axis_index("dp")
    pos, width = cot.shape
    sl = width // n
    rows = width // nb
    pieces = tq.shape[1]
    half = sl // pieces
    main = sl // 128 * 128
    ny, outer = n // 2, nb // 2
    y, c = me // 2, me % 2
    mate = y * 2 + 1 - c
    oz, ox = dp // 2, dp % 2
    scale = HD ** (-0.5)

    loads = [
        pltpu.make_async_copy(cot_hbm, cot, loc_sem.at[0]),
        pltpu.make_async_copy(sqkv_hbm, sqkv, loc_sem.at[1]),
        pltpu.make_async_copy(tqkv_hbm, tqkv, loc_sem.at[2]),
        pltpu.make_async_copy(proj_hbm.at[me], proj, loc_sem.at[3]),
    ]
    for load in loads:
        load.start()
    barrier = pltpu.get_barrier_semaphore()
    for j in range(1, n):
        pl.semaphore_signal(barrier, inc=1, device_id=(dp, (me + j) % n), device_id_type=MESH)
    pl.semaphore_signal(barrier, inc=1, device_id=(oz * 2 + 1 - ox, me), device_id_type=MESH)
    for j in range(1, outer):
        pl.semaphore_signal(
            barrier, inc=1, device_id=((oz + j) % outer * 2 + ox, me), device_id_type=MESH
        )

    def remote(src, dst, s_sem, r_sem, to):
        return pltpu.make_async_remote_copy(
            src_ref=src, dst_ref=dst, send_sem=s_sem, recv_sem=r_sem, device_id=to,
            device_id_type=MESH,
        )

    def turned(value):
        return value.astype(F32).T

    loads[0].wait()
    cot_t[me] = turned(cot[...]).astype(BF16)
    pl.semaphore_wait(barrier, (n - 1) + 1 + (outer - 1))

    sent = []

    def send(copy):
        copy.start()
        sent.append(copy)

    def y_copy(j):
        return remote(
            cot_t.at[me], cot_t.at[me], cs.at[j - 1], cr.at[j - 1], (dp, (y + j) % ny * 2 + c)
        )

    def pass_copy(j, core):
        slot = (y + ny - j) % ny * 2 + core
        return remote(cot_t.at[slot], cot_t.at[slot], fs.at[j], fr.at[j], (dp, mate))

    for j in range(1, ny):
        send(y_copy(j))
    send(pass_copy(0, c))

    live_frames = counts[0, 0]
    live_positions = counts[0, 1]

    loads[1].wait()
    q_t[...] = turned(sqkv[0])
    v_t[...] = turned(sqkv[2])
    key_keep = lax.broadcasted_iota(jnp.int32, (pos, pos), 0) < live_positions
    for h in range(HEADS):
        low = h * HD
        w0 = low // 128 * 128
        w1 = -(-(low + HD) // 128) * 128
        row = lax.broadcasted_iota(jnp.int32, (w1 - w0, pos), 0)
        inside = (row >= low - w0) & (row < low - w0 + HD)
        q_win = jnp.where(inside, q_t[w0:w1, :], 0.0).astype(BF16)
        scores = jnp.dot(sqkv[1, :, w0:w1], q_win, preferred_element_type=F32) * scale
        scores = jnp.where(key_keep, scores, -1e30)
        expo = jnp.exp(scores - jnp.max(scores, axis=0, keepdims=True))
        weights = (expo / jnp.sum(expo, axis=0, keepdims=True)).astype(BF16)
        o_t[low : low + HD, :] = jnp.dot(
            v_t[low : low + HD, :].astype(BF16), weights, preferred_element_type=F32
        )
    for s in range(n):
        so[s, 0] = o_t[s * sl : (s + 1) * sl, :].astype(BF16)
    so_r[me] = so[me]

    def swap(src, dst, s_sem, r_sem, i=0):
        for j in range(1, n):
            to = (me + j) % n
            send(
                remote(
                    src.at[to, i], dst.at[me, i], s_sem.at[i, j - 1], r_sem.at[i, j - 1], (dp, to)
                )
            )

    def arrive(src, dst, s_sem, r_sem, i=0):
        for j in range(1, n):
            origin = (me + n - j) % n
            remote(
                src.at[origin, i], dst.at[origin, i], s_sem.at[i, j - 1], r_sem.at[i, j - 1],
                (dp, origin),
            ).wait_recv()

    swap(so, so_r, ss, sr)

    loads[2].wait()
    for m in range(3):
        flat = turned(tqkv[m]).astype(BF16)
        for s in range(n):
            for i in range(pieces):
                low = s * sl + i * half
                tq[s, i, m] = flat[low : low + half, :]
    tq_r[me] = tq[me]
    for i in range(pieces):
        swap(tq, tq_r, ts, tr, i)

    def gate_rows(gate):
        return jnp.broadcast_to(gate[...], (pos, width)).T

    for j in range(1, ny):
        slot = (y + ny - j) % ny * 2 + c
        remote(
            cot_t.at[slot], cot_t.at[slot], cs.at[j - 1], cr.at[j - 1], (dp, mate)
        ).wait_recv()
        send(pass_copy(j, c))
    for j in range(ny):
        pass_copy(j, 1 - c).wait_recv()

    lane = lax.broadcasted_iota(jnp.int32, (1, pos), 1)
    keep = [
        ((lane < live_positions) & (f < live_frames)).astype(F32) for f in range(n)
    ]

    def errors(target, gate):
        columns = gate_rows(gate)
        for f in range(n):
            target[:, f * pos : (f + 1) * pos] = (
                keep[f] * cot_t[f].astype(F32) * columns
            ).astype(BF16)

    order = list(range(1, outer)) + [0]

    def times(left, right):
        return lax.dot_general(left, right, (((1,), (1,)), ((), ())), preferred_element_type=F32)

    def product(p, source, outs):
        tail = sl - main
        if tail:
            short = rows // groups
            edges = []
            for k in range(groups):
                blank = [
                    jnp.zeros((size, outs.shape[1]), BF16)
                    for size in (k * tail, 128 - (k + 1) * tail)
                ]
                parts = [blank[0], outs[main:, :], blank[1]]
                edges.append(jnp.concatenate([v for v in parts if v.shape[0]], axis=0))
        for x in (1 - ox, ox):
            for j in order:
                d = (oz + j) % outer * 2 + x
                first = pl.multiple_of(d * rows, 16)
                wide = times(source[pl.ds(first, rows), :], outs[:main, :]).astype(BF16)
                for k in range(main // 128):
                    part[p, d, k * rows : (k + 1) * rows, :] = wide[:, k * 128 : (k + 1) * 128]
                if tail:
                    edge = functools.reduce(
                        jnp.add,
                        [
                            times(
                                source[pl.ds(pl.multiple_of(first + k * short, 16), short), :],
                                edges[k],
                            )
                            for k in range(groups)
                        ],
                    )
                    part[p, d, main // 128 * rows :, :] = edge.astype(BF16)
                if x is not ox:
                    send(pair_copy(p, j))

    def pair_copy(p, j):
        z = (oz + j) % outer
        return remote(
            part.at[p, z * 2 + 1 - ox], xr.at[p, j], xss.at[p, j], xrs.at[p, j],
            (oz * 2 + 1 - ox, me),
        )

    def line_copy(p, j):
        z = (oz + j) % outer
        return remote(
            zs.at[p, j - 1], zr.at[p, j - 1], zss.at[p, j - 1], zrs.at[p, j - 1], (z * 2 + ox, me)
        )

    def line_start(p):
        for j in order:
            z = (oz + j) % outer
            pair_copy(p, j).wait_recv()
            if j:
                zs[p, j - 1] = (
                    part[p, z * 2 + ox].astype(F32) + xr[p, j].astype(F32)
                ).astype(BF16)
                send(line_copy(p, j))

    def line_end(p):
        total = part[p, oz * 2 + ox].astype(F32) + xr[p, 0].astype(F32)
        for j in range(1, outer):
            line_copy(p, j).wait_recv()
            total = total + zr[p, j - 1].astype(F32)
        sum_out[p] = total

    errors(err, sgate)
    arrive(so, so_r, ss, sr)
    product(0, err, jnp.concatenate([so_r[f, 0] for f in range(n)], axis=1))

    errors(err2, tgate)
    loads[3].wait()
    do_t[...] = (
        jnp.dot(proj[...], err2[...], preferred_element_type=F32).astype(BF16).astype(F32)
    )
    line_start(0)

    heads = half // HD

    def forward(i):
        kept = []
        for f in range(n):
            for m in range(3):
                tqf[f, i, m] = tq_r[f, i, m].astype(F32)
        for h in range(heads):
            band = slice(h * HD, (h + 1) * HD)
            place = slice(i * half + h * HD, i * half + (h + 1) * HD)
            ks = [tqf[g, i, 1, band, :] for g in range(n)]
            vs = [tqf[g, i, 2, band, :] for g in range(n)]
            for f in range(n):
                q = tqf[f, i, 0, band, :]
                row = [
                    jnp.where(
                        g < live_frames, jnp.sum(q * ks[g], axis=0, keepdims=True) * scale, -1e30
                    )
                    for g in range(n)
                ]
                top = functools.reduce(jnp.maximum, row)
                expo = [jnp.exp(value - top) for value in row]
                total = functools.reduce(jnp.add, expo)
                soft = [value / total for value in expo]
                rounded = [value.astype(BF16).astype(F32) for value in soft]
                kept.append((soft, rounded))
                ot[place, f * pos : (f + 1) * pos] = functools.reduce(
                    jnp.add, [rounded[g] * vs[g] for g in range(n)]
                )
        return kept

    def backward(i, kept):
        for h in range(heads):
            band = slice(h * HD, (h + 1) * HD)
            place = slice(i * half + h * HD, i * half + (h + 1) * HD)
            backs = [do_t[place, f * pos : (f + 1) * pos] for f in range(n)]
            slopes = []
            for f in range(n):
                soft, _ = kept[h * n + f]
                dw = [
                    jnp.sum(backs[f] * tqf[g, i, 2, band, :], axis=0, keepdims=True)
                    .astype(BF16)
                    .astype(F32)
                    for g in range(n)
                ]
                mean = functools.reduce(jnp.add, [soft[g] * dw[g] for g in range(n)])
                slopes.append([soft[g] * (dw[g] - mean) * scale for g in range(n)])
            for f in range(n):
                gf[f, i, 0, band, :] = functools.reduce(
                    jnp.add, [slopes[f][g] * tqf[g, i, 1, band, :] for g in range(n)]
                )
                gf[f, i, 1, band, :] = functools.reduce(
                    jnp.add, [slopes[g][f] * tqf[g, i, 0, band, :] for g in range(n)]
                )
                gf[f, i, 2, band, :] = functools.reduce(
                    jnp.add, [kept[h * n + g][1][f] * backs[g] for g in range(n)]
                )
        for f in range(n):
            for m in range(3):
                gs[f, i, m] = gf[f, i, m].astype(BF16)
        swap(gs, gr, us, ur, i)

    for i in range(pieces):
        arrive(tq, tq_r, ts, tr, i)
        kept = forward(i)
        if i == pieces - 1:
            product(1, err2, ot[...].astype(BF16))
        backward(i, kept)
    gr[me] = gs[me]

    line_end(0)
    line_start(1)
    for i in range(pieces):
        arrive(gs, gr, us, ur, i)
        for s in range(n):
            for m in range(3):
                low = s * sl + i * half
                g_out[m, low : low + half, :] = gr[s, i, m]
    line_end(1)
    for copy in sent:
        copy.wait_send()


def finish(nb, groups, grads, sums, g_out, sp_out, tp_out):
    g_out[0] = grads[0].astype(F32).T.astype(BF16)
    rows, sl = sp_out.shape
    main, short = sl // 128 * 128, rows // groups
    tail = sl - main

    @pl.when(pl.program_id(0) == 0)
    def _():
        for p, out in enumerate((sp_out, tp_out)):
            for k in range(main // 128):
                out[:, k * 128 : (k + 1) * 128] = sums[p, k * rows : (k + 1) * rows, :]
            if tail:
                edge = sums[p, main // 128 * rows :, :]
                for k in range(groups):
                    out[k * short : (k + 1) * short, main:] = edge[:, k * tail : (k + 1) * tail]


def kernel_body(
    n, nb, spatial_qkv, temporal_qkv, cotangent, spatial_gate, temporal_gate, temporal_proj, live_counts
):
    pos, width = cotangent.shape[2:]
    sl, rows, outer, ny = width // n, width // nb, nb // 2, n // 2
    vm, dma = pltpu.VMEM, pltpu.SemaphoreType.DMA
    whole = pl.BlockSpec(memory_space=pltpu.VMEM)
    left = pl.BlockSpec(memory_space=pl.ANY)
    pieces = 2 if sl // HD % 2 == 0 and sl // 2 % 16 == 0 else 1
    half, tail = sl // pieces, sl % 128
    groups = 1
    if tail:
        groups = max(g for g in range(1, 128 // tail + 1) if rows % (16 * g) == 0)
    packed = sl // 128 * rows + (rows // groups if tail else 0)
    grads, sums = pl.pallas_call(
        functools.partial(kernel, n, nb, groups),
        out_shape=(
            jax.ShapeDtypeStruct((3, width, pos), BF16),
            jax.ShapeDtypeStruct((2, packed, 128), F32),
        ),
        in_specs=[pl.BlockSpec(memory_space=pltpu.SMEM), whole, whole, left, left, left, left],
        out_specs=(whole, whole),
        scratch_shapes=[
            vm((3, pos, width), BF16), vm((3, pos, width), BF16), vm((pos, width), BF16),
            vm((sl, width), BF16), vm((n, width, pos), BF16),
            vm((width, pos), F32), vm((width, pos), F32), vm((width, pos), F32),
            vm((n, 1, sl, pos), BF16), vm((n, 1, sl, pos), BF16),
            vm((n, pieces, 3, half, pos), BF16), vm((n, pieces, 3, half, pos), BF16),
            vm((n, pieces, 3, half, pos), F32), vm((n, pieces, 3, half, pos), F32),
            vm((width, n * pos), BF16), vm((width, n * pos), BF16),
            vm((sl, n * pos), F32), vm((sl, n * pos), F32),
            vm((2, nb, packed, 128), BF16), vm((2, outer, packed, 128), BF16),
            vm((2, outer - 1, packed, 128), BF16), vm((2, outer - 1, packed, 128), BF16),
            vm((n, pieces, 3, half, pos), BF16), vm((n, pieces, 3, half, pos), BF16),
            dma((4,)), dma((ny - 1,)), dma((ny - 1,)), dma((ny,)), dma((ny,)),
            dma((1, n - 1)), dma((1, n - 1)), dma((pieces, n - 1)), dma((pieces, n - 1)),
            dma((pieces, n - 1)), dma((pieces, n - 1)),
            dma((2, outer)), dma((2, outer)), dma((2, outer - 1)), dma((2, outer - 1)),
        ],
        compiler_params=pltpu.CompilerParams(
            collective_id=0, has_side_effects=True, vmem_limit_bytes=56 * 1024 * 1024
        ),
    )(
        live_counts, spatial_gate, temporal_gate,
        spatial_qkv.reshape(3, pos, width), temporal_qkv.reshape(3, pos, width),
        cotangent.reshape(pos, width), temporal_proj.reshape(n, sl, width),
    )
    fixed = lambda i: (0, 0)
    grads, first, second = pl.pallas_call(
        functools.partial(finish, nb, groups),
        grid=(3,),
        out_shape=(
            jax.ShapeDtypeStruct((3, pos, width), BF16),
            jax.ShapeDtypeStruct((rows, sl), F32),
            jax.ShapeDtypeStruct((rows, sl), F32),
        ),
        in_specs=[
            pl.BlockSpec((1, width, pos), lambda i: (i, 0, 0)),
            pl.BlockSpec((2, packed, 128), lambda i: (0, 0, 0)),
        ],
        out_specs=(
            pl.BlockSpec((1, pos, width), lambda i: (i, 0, 0)),
            pl.BlockSpec((rows, sl), fixed),
            pl.BlockSpec((rows, sl), fixed),
        ),
    )(grads, sums)
    return grads[None, :, None], first.T, second.T


def solution(mesh):
    n, nb = mesh.shape["seq"], mesh.shape["dp"]

    def chosen(*args):
        cot = args[2]
        _, frames, pos, width = cot.shape
        fits = frames == 1 and pos == 128 and width == HEADS * HD and n % 2 == 0 and nb % 2 == 0
        fits = fits and n > 2 and nb > 2 and HEADS % n == 0
        if fits and width // n % 16 == 0 and width // nb % 16 == 0:
            return kernel_body(n, nb, *args)
        return body(*args)

    return jax.shard_map(
        chosen,
        mesh=mesh,
        in_specs=(
            P("dp", None, "seq", None, None),
            P("dp", None, "seq", None, None),
            P("dp", "seq", None, None),
            P("dp", None),
            P("dp", None),
            P(),
            P("dp", None),
        ),
        out_specs=(P("dp", None, "seq", None, None), P("seq", "dp"), P("seq", "dp")),
        check_vma=False,
    )
```

```python
import functools

import jax
import jax.numpy as jnp
from jax import lax
from jax.experimental import pallas as pl
from jax.experimental.pallas import tpu as pltpu
from jax.sharding import PartitionSpec as P

HEADS = 16
HD = 72
MESH = pl.DeviceIdType.MESH
F32 = jnp.float32
BF16 = jnp.bfloat16


def attend(queries, key_block, value_block, key_keep, score_form, mix_form):
    head_split = queries.shape[:-1] + (HEADS, HD)
    q_heads = queries.reshape(head_split)
    k_heads = key_block.reshape(head_split)
    v_heads = value_block.reshape(head_split)
    scores = jnp.einsum(score_form, q_heads, k_heads, preferred_element_type=jnp.float32) * HD ** (
        -0.5
    )
    scores = jnp.where(key_keep[:, None, None, :], scores, -1e30)
    shifted = scores - jnp.max(scores, axis=-1, keepdims=True)
    expo = jnp.exp(shifted)
    attention_weights = (expo / jnp.sum(expo, axis=-1, keepdims=True)).astype(jnp.bfloat16)
    mixed = jnp.einsum(mix_form, attention_weights, v_heads, preferred_element_type=jnp.float32)
    return mixed.reshape(queries.shape)


def body(
    spatial_qkv, temporal_qkv, cotangent, spatial_gate, temporal_gate, temporal_proj, live_counts
):
    spatial = spatial_qkv[0]
    temporal = temporal_qkv[0]
    incoming = cotangent[0]
    frame_count, position_count, width = incoming.shape
    group_size = lax.axis_size("seq")
    member = lax.axis_index("seq")
    live_frames = live_counts[0, 0]
    live_positions = live_counts[0, 1]
    frame_ids = member * frame_count + jnp.arange(frame_count, dtype=jnp.int32)
    position_ids = jnp.arange(position_count, dtype=jnp.int32)
    token_mask = (
        (frame_ids[:, None] < live_frames) & (position_ids[None, :] < live_positions)
    ).astype(jnp.float32)
    flowing = token_mask[:, :, None] * incoming.astype(jnp.float32)
    temporal_error = (flowing * temporal_gate[0]).astype(jnp.bfloat16)
    temporal_back = lax.dot_general(
        temporal_error, temporal_proj, (((2,), (1,)), ((), ())), preferred_element_type=jnp.float32
    ).astype(jnp.bfloat16)
    stacked = jnp.concatenate([temporal, temporal_back[None]], axis=0)
    exchanged = lax.all_to_all(stacked, "seq", split_axis=2, concat_axis=1, tiled=True)
    spatial_keep = position_ids[None, :] < live_positions
    spatial_out = attend(
        spatial[0], spatial[1], spatial[2], spatial_keep, "bqhd,bkhd->bhqk", "bhqk,bkhd->bqhd"
    ).astype(jnp.bfloat16)
    total_frames = exchanged.shape[1]
    slice_positions = exchanged.shape[2]
    temporal_keep = jnp.broadcast_to(
        jnp.arange(total_frames, dtype=jnp.int32)[None, :] < live_frames,
        (slice_positions, total_frames),
    )

    def temporal_attend(queries, key_block, value_block):
        return attend(
            queries, key_block, value_block, temporal_keep, "qbhd,kbhd->bhqk", "bhqk,kbhd->qbhd"
        )

    temporal_result, pullback = jax.vjp(temporal_attend, exchanged[0], exchanged[1], exchanged[2])
    temporal_out = temporal_result.astype(jnp.bfloat16)
    input_grads = jnp.stack(pullback(exchanged[3].astype(jnp.float32)))
    temporal_frames = lax.all_to_all(temporal_out, "seq", split_axis=0, concat_axis=1, tiled=True)
    grads_home = lax.all_to_all(input_grads, "seq", split_axis=1, concat_axis=2, tiled=True)
    tokens = frame_count * position_count
    flat_spatial = spatial_out.reshape(tokens, width)
    flat_temporal = temporal_frames.reshape(tokens, width)
    slice_width = width // group_size
    column_spatial, column_temporal = (
        lax.all_to_all(flat_spatial, "seq", split_axis=1, concat_axis=0, tiled=True),
        lax.all_to_all(flat_temporal, "seq", split_axis=1, concat_axis=0, tiled=True),
    )
    spatial_scale = spatial_gate[0]
    temporal_scale = temporal_gate[0]
    starting = jnp.zeros((slice_width, 2, width), jnp.float32)
    cot_piece = lax.all_gather(incoming.reshape(tokens, width), "seq", axis=0, tiled=True)
    shards = cot_piece.shape[0] // tokens

    def one_block(block, total):
        offset = (block * tokens).astype(jnp.int32)
        rows = lax.dynamic_slice_in_dim(cot_piece, offset, tokens, 0)
        token_index = offset + jnp.arange(tokens, dtype=jnp.int32)
        frame_of = token_index // position_count
        position_of = token_index % position_count
        row_keep = ((frame_of < live_frames) & (position_of < live_positions)).astype(jnp.float32)
        masked_rows = row_keep[:, None] * rows.astype(jnp.float32)
        error_first = (masked_rows * spatial_scale).astype(jnp.bfloat16)
        error_second = (masked_rows * temporal_scale).astype(jnp.bfloat16)
        cols_first = lax.dynamic_slice_in_dim(column_spatial, offset, tokens, 0)
        cols_second = lax.dynamic_slice_in_dim(column_temporal, offset, tokens, 0)
        part_first = lax.dot_general(
            cols_first, error_first, (((0,), (0,)), ((), ())), preferred_element_type=jnp.float32
        )
        part_second = lax.dot_general(
            cols_second, error_second, (((0,), (0,)), ((), ())), preferred_element_type=jnp.float32
        )
        part_first = part_first.astype(jnp.bfloat16).astype(jnp.float32)
        part_second = part_second.astype(jnp.bfloat16).astype(jnp.float32)
        return total + jnp.stack([part_first, part_second], axis=1)

    partial_sum = lax.fori_loop(0, shards, one_block, starting)
    summed = lax.psum_scatter(partial_sum, "dp", scatter_dimension=2, tiled=True)
    return (grads_home[None], summed[:, 0], summed[:, 1])


def kernel(
    n, nb, units, counts, sgate, tgate, sqkv_hbm, tqkv_hbm, cot_hbm, proj_hbm,
    g_out, sum_out,
    sqkv, tqkv, cot, proj, cot_t, q_t, v_t, o_t, so, so_r, tq, tq_r, tqf, gf,
    err, err2, ot, do_t, part, xr, zs, zr, gs, gr,
    loc_sem, cs, cr, fs, fr, ss, sr, ts, tr, us, ur, xss, xrs, zss, zrs,
):
    me = lax.axis_index("seq")
    dp = lax.axis_index("dp")
    pos, width = cot.shape
    sl = width // n
    rows = width // nb
    pieces = tq.shape[1]
    half = sl // pieces
    ny, outer = n // 2, nb // 2
    y, c = me // 2, me % 2
    mate = y * 2 + 1 - c
    oz, ox = dp // 2, dp % 2
    scale = HD ** (-0.5)

    loads = [
        pltpu.make_async_copy(cot_hbm, cot, loc_sem.at[0]),
        pltpu.make_async_copy(sqkv_hbm, sqkv, loc_sem.at[1]),
        pltpu.make_async_copy(tqkv_hbm, tqkv, loc_sem.at[2]),
        pltpu.make_async_copy(proj_hbm.at[me], proj, loc_sem.at[3]),
    ]
    for load in loads:
        load.start()
    barrier = pltpu.get_barrier_semaphore()
    for j in range(1, n):
        pl.semaphore_signal(barrier, inc=1, device_id=(dp, (me + j) % n), device_id_type=MESH)
    pl.semaphore_signal(barrier, inc=1, device_id=(oz * 2 + 1 - ox, me), device_id_type=MESH)
    for j in range(1, outer):
        pl.semaphore_signal(
            barrier, inc=1, device_id=((oz + j) % outer * 2 + ox, me), device_id_type=MESH
        )

    def remote(src, dst, s_sem, r_sem, to):
        return pltpu.make_async_remote_copy(
            src_ref=src, dst_ref=dst, send_sem=s_sem, recv_sem=r_sem, device_id=to,
            device_id_type=MESH,
        )

    def turned(value):
        return value.astype(F32).T

    loads[0].wait()
    cot_t[me] = turned(cot[...]).astype(BF16)
    pl.semaphore_wait(barrier, (n - 1) + 1 + (outer - 1))

    sent = []

    def send(copy):
        copy.start()
        sent.append(copy)

    def y_copy(j):
        return remote(
            cot_t.at[me], cot_t.at[me], cs.at[j - 1], cr.at[j - 1], (dp, (y + j) % ny * 2 + c)
        )

    def pass_copy(j, core):
        slot = (y + ny - j) % ny * 2 + core
        return remote(cot_t.at[slot], cot_t.at[slot], fs.at[j], fr.at[j], (dp, mate))

    for j in range(1, ny):
        send(y_copy(j))
    send(pass_copy(0, c))

    live_frames = counts[0, 0]
    live_positions = counts[0, 1]

    loads[1].wait()
    q_t[...] = turned(sqkv[0])
    v_t[...] = turned(sqkv[2])
    key_keep = lax.broadcasted_iota(jnp.int32, (pos, pos), 0) < live_positions
    for h in range(HEADS):
        low = h * HD
        w0 = low // 128 * 128
        w1 = -(-(low + HD) // 128) * 128
        row = lax.broadcasted_iota(jnp.int32, (w1 - w0, pos), 0)
        inside = (row >= low - w0) & (row < low - w0 + HD)
        q_win = jnp.where(inside, q_t[w0:w1, :], 0.0).astype(BF16)
        scores = jnp.dot(sqkv[1, :, w0:w1], q_win, preferred_element_type=F32) * scale
        scores = jnp.where(key_keep, scores, -1e30)
        expo = jnp.exp(scores - jnp.max(scores, axis=0, keepdims=True))
        weights = (expo / jnp.sum(expo, axis=0, keepdims=True)).astype(BF16)
        o_t[low : low + HD, :] = jnp.dot(
            v_t[low : low + HD, :].astype(BF16), weights, preferred_element_type=F32
        )
    for s in range(n):
        so[s, 0] = o_t[s * sl : (s + 1) * sl, :].astype(BF16)
    so_r[me] = so[me]

    def swap(src, dst, s_sem, r_sem, i=0):
        for j in range(1, n):
            to = (me + j) % n
            send(
                remote(
                    src.at[to, i], dst.at[me, i], s_sem.at[i, j - 1], r_sem.at[i, j - 1], (dp, to)
                )
            )

    def arrive(src, dst, s_sem, r_sem, i=0):
        for j in range(1, n):
            origin = (me + n - j) % n
            remote(
                src.at[origin, i], dst.at[origin, i], s_sem.at[i, j - 1], r_sem.at[i, j - 1],
                (dp, origin),
            ).wait_recv()

    swap(so, so_r, ss, sr)

    loads[2].wait()
    for m in range(3):
        flat = turned(tqkv[m]).astype(BF16)
        for s in range(n):
            for i in range(pieces):
                low = s * sl + i * half
                tq[s, i, m] = flat[low : low + half, :]
    tq_r[me] = tq[me]
    for i in range(pieces):
        swap(tq, tq_r, ts, tr, i)

    def gate_rows(gate):
        return jnp.broadcast_to(gate[...], (pos, width)).T

    for j in range(1, ny):
        slot = (y + ny - j) % ny * 2 + c
        remote(
            cot_t.at[slot], cot_t.at[slot], cs.at[j - 1], cr.at[j - 1], (dp, mate)
        ).wait_recv()
        send(pass_copy(j, c))
    for j in range(ny):
        pass_copy(j, 1 - c).wait_recv()

    lane = lax.broadcasted_iota(jnp.int32, (1, pos), 1)
    keep = [
        ((lane < live_positions) & (f < live_frames)).astype(F32) for f in range(n)
    ]

    def errors(target, gate):
        columns = gate_rows(gate)
        for f in range(n):
            target[:, f * pos : (f + 1) * pos] = (
                keep[f] * cot_t[f].astype(F32) * columns
            ).astype(BF16)

    order = list(range(1, outer)) + [0]

    def times(left, right):
        return lax.dot_general(left, right, (((1,), (1,)), ((), ())), preferred_element_type=F32)

    def product(p, source, outs):
        main, tail, groups, _ = units[p]
        if tail:
            short = rows // groups
            edges = []
            for k in range(groups):
                blank = [
                    jnp.zeros((size, outs.shape[1]), BF16)
                    for size in (k * tail, 128 - (k + 1) * tail)
                ]
                parts = [blank[0], outs[main:, :], blank[1]]
                edges.append(jnp.concatenate([v for v in parts if v.shape[0]], axis=0))
        for x in (1 - ox, ox):
            for j in order:
                d = (oz + j) % outer * 2 + x
                first = pl.multiple_of(d * rows, 16)
                wide = times(source[pl.ds(first, rows), :], outs[:main, :]).astype(BF16)
                for k in range(main // 128):
                    part[p, d, k * rows : (k + 1) * rows, :] = wide[:, k * 128 : (k + 1) * 128]
                if tail:
                    edge = functools.reduce(
                        jnp.add,
                        [
                            times(
                                source[pl.ds(pl.multiple_of(first + k * short, 16), short), :],
                                edges[k],
                            )
                            for k in range(groups)
                        ],
                    )
                    part[p, d, main // 128 * rows : units[p][3], :] = edge.astype(BF16)
                if x is not ox:
                    send(pair_copy(p, j))

    def pair_copy(p, j):
        z = (oz + j) % outer
        return remote(
            part.at[p, z * 2 + 1 - ox, : units[p][3]], xr.at[p, j, : units[p][3]], xss.at[p, j], xrs.at[p, j],
            (oz * 2 + 1 - ox, me),
        )

    def line_copy(p, j):
        z = (oz + j) % outer
        return remote(
            zs.at[p, j - 1, : units[p][3]], zr.at[p, j - 1, : units[p][3]],
            zss.at[p, j - 1], zrs.at[p, j - 1], (z * 2 + ox, me)
        )

    def line_start(p):
        for j in order:
            z = (oz + j) % outer
            pair_copy(p, j).wait_recv()
            if j:
                size = units[p][3]
                zs[p, j - 1, :size, :] = (
                    part[p, z * 2 + ox, :size, :].astype(F32) + xr[p, j, :size, :].astype(F32)
                ).astype(BF16)
                send(line_copy(p, j))

    def line_end(p):
        size = units[p][3]
        total = part[p, oz * 2 + ox, :size, :].astype(F32) + xr[p, 0, :size, :].astype(F32)
        for j in range(1, outer):
            line_copy(p, j).wait_recv()
            total = total + zr[p, j - 1, :size, :].astype(F32)
        sum_out[p, :size, :] = total

    errors(err, sgate)
    arrive(so, so_r, ss, sr)
    product(0, err, jnp.concatenate([so_r[f, 0] for f in range(n)], axis=1))

    errors(err2, tgate)
    loads[3].wait()
    do_t[...] = (
        jnp.dot(proj[...], err2[...], preferred_element_type=F32).astype(BF16).astype(F32)
    )
    heads = half // HD

    def forward(i):
        kept = []
        for f in range(n):
            for m in range(3):
                tqf[f, i, m] = tq_r[f, i, m].astype(F32)
        for h in range(heads):
            band = slice(h * HD, (h + 1) * HD)
            place = slice(i * half + h * HD, i * half + (h + 1) * HD)
            ks = [tqf[g, i, 1, band, :] for g in range(n)]
            vs = [tqf[g, i, 2, band, :] for g in range(n)]
            for f in range(n):
                q = tqf[f, i, 0, band, :]
                row = [
                    jnp.where(
                        g < live_frames, jnp.sum(q * ks[g], axis=0, keepdims=True) * scale, -1e30
                    )
                    for g in range(n)
                ]
                top = functools.reduce(jnp.maximum, row)
                expo = [jnp.exp(value - top) for value in row]
                total = functools.reduce(jnp.add, expo)
                soft = [value / total for value in expo]
                rounded = [value.astype(BF16).astype(F32) for value in soft]
                kept.append((soft, rounded))
                ot[place, f * pos : (f + 1) * pos] = functools.reduce(
                    jnp.add, [rounded[g] * vs[g] for g in range(n)]
                )
        return kept

    def backward(i, kept):
        for h in range(heads):
            band = slice(h * HD, (h + 1) * HD)
            place = slice(i * half + h * HD, i * half + (h + 1) * HD)
            backs = [do_t[place, f * pos : (f + 1) * pos] for f in range(n)]
            slopes = []
            for f in range(n):
                soft, _ = kept[h * n + f]
                dw = [
                    jnp.sum(backs[f] * tqf[g, i, 2, band, :], axis=0, keepdims=True)
                    .astype(BF16)
                    .astype(F32)
                    for g in range(n)
                ]
                mean = functools.reduce(jnp.add, [soft[g] * dw[g] for g in range(n)])
                slopes.append([soft[g] * (dw[g] - mean) * scale for g in range(n)])
            for f in range(n):
                gf[f, i, 0, band, :] = functools.reduce(
                    jnp.add, [slopes[f][g] * tqf[g, i, 1, band, :] for g in range(n)]
                )
                gf[f, i, 1, band, :] = functools.reduce(
                    jnp.add, [slopes[g][f] * tqf[g, i, 0, band, :] for g in range(n)]
                )
                gf[f, i, 2, band, :] = functools.reduce(
                    jnp.add, [kept[h * n + g][1][f] * backs[g] for g in range(n)]
                )
        for f in range(n):
            for m in range(3):
                gs[f, i, m] = gf[f, i, m].astype(BF16)
        swap(gs, gr, us, ur, i)

    for i in range(pieces):
        arrive(tq, tq_r, ts, tr, i)
        kept = forward(i)
        product(1 + i, err2, ot[i * half : (i + 1) * half, :].astype(BF16))
        backward(i, kept)
        if i == 0:
            line_start(0)
    gr[me] = gs[me]

    line_end(0)
    for i in range(pieces):
        line_start(1 + i)
    for i in range(pieces):
        arrive(gs, gr, us, ur, i)
    for m in range(3):
        for s in range(n):
            for i in range(pieces):
                low = s * sl + i * half
                q_t[low : low + half, :] = gr[s, i, m].astype(F32)
        g_out[m] = q_t[...].T.astype(BF16)
    for i in range(pieces):
        line_end(1 + i)
    for copy in sent:
        copy.wait_send()


def finish(units, grads, sums, g_out, sp_out, tp_out):
    g_out[...] = grads[...]
    rows = sp_out.shape[0]

    @pl.when(pl.program_id(0) == 0)
    def _():
        left = 0
        for p, (main, tail, groups, size) in enumerate(units):
            out = tp_out if p else sp_out
            for k in range(main // 128):
                low = left + k * 128
                out[:, low : low + 128] = sums[p, k * rows : (k + 1) * rows, :]
            if tail:
                short = rows // groups
                edge = sums[p, main // 128 * rows : size, :]
                low = left + main
                for k in range(groups):
                    out[k * short : (k + 1) * short, low : low + tail] = edge[
                        :, k * tail : (k + 1) * tail
                    ]
            left = left + main + tail if p else 0


def unit_of(columns, rows):
    main, tail = columns // 128 * 128, columns % 128
    groups = 1
    if tail:
        groups = max(g for g in range(1, 128 // tail + 1) if rows % (16 * g) == 0)
    return main, tail, groups, main // 128 * rows + (rows // groups if tail else 0)


def kernel_body(
    n, nb, spatial_qkv, temporal_qkv, cotangent, spatial_gate, temporal_gate, temporal_proj, live_counts
):
    pos, width = cotangent.shape[2:]
    sl, rows, outer, ny = width // n, width // nb, nb // 2, n // 2
    vm, dma = pltpu.VMEM, pltpu.SemaphoreType.DMA
    whole = pl.BlockSpec(memory_space=pltpu.VMEM)
    left = pl.BlockSpec(memory_space=pl.ANY)
    pieces = 2 if sl // HD % 2 == 0 and sl // 2 % 16 == 0 else 1
    half = sl // pieces
    units = [unit_of(sl, rows)] + [unit_of(half, rows)] * pieces
    count, packed = len(units), max(unit[3] for unit in units)
    grads, sums = pl.pallas_call(
        functools.partial(kernel, n, nb, units),
        out_shape=(
            jax.ShapeDtypeStruct((3, pos, width), BF16),
            jax.ShapeDtypeStruct((count, packed, 128), F32),
        ),
        in_specs=[pl.BlockSpec(memory_space=pltpu.SMEM), whole, whole, left, left, left, left],
        out_specs=(whole, whole),
        scratch_shapes=[
            vm((3, pos, width), BF16), vm((3, pos, width), BF16), vm((pos, width), BF16),
            vm((sl, width), BF16), vm((n, width, pos), BF16),
            vm((width, pos), F32), vm((width, pos), F32), vm((width, pos), F32),
            vm((n, 1, sl, pos), BF16), vm((n, 1, sl, pos), BF16),
            vm((n, pieces, 3, half, pos), BF16), vm((n, pieces, 3, half, pos), BF16),
            vm((n, pieces, 3, half, pos), F32), vm((n, pieces, 3, half, pos), F32),
            vm((width, n * pos), BF16), vm((width, n * pos), BF16),
            vm((sl, n * pos), F32), vm((sl, n * pos), F32),
            vm((count, nb, packed, 128), BF16), vm((count, outer, packed, 128), BF16),
            vm((count, outer - 1, packed, 128), BF16), vm((count, outer - 1, packed, 128), BF16),
            vm((n, pieces, 3, half, pos), BF16), vm((n, pieces, 3, half, pos), BF16),
            dma((4,)), dma((ny - 1,)), dma((ny - 1,)), dma((ny,)), dma((ny,)),
            dma((1, n - 1)), dma((1, n - 1)), dma((pieces, n - 1)), dma((pieces, n - 1)),
            dma((pieces, n - 1)), dma((pieces, n - 1)),
            dma((count, outer)), dma((count, outer)), dma((count, outer - 1)), dma((count, outer - 1)),
        ],
        compiler_params=pltpu.CompilerParams(
            collective_id=0, has_side_effects=True, vmem_limit_bytes=56 * 1024 * 1024
        ),
    )(
        live_counts, spatial_gate, temporal_gate,
        spatial_qkv.reshape(3, pos, width), temporal_qkv.reshape(3, pos, width),
        cotangent.reshape(pos, width), temporal_proj.reshape(n, sl, width),
    )
    fixed = lambda i: (0, 0)
    grads, first, second = pl.pallas_call(
        functools.partial(finish, units),
        grid=(3,),
        out_shape=(
            jax.ShapeDtypeStruct((3, pos, width), BF16),
            jax.ShapeDtypeStruct((rows, sl), F32),
            jax.ShapeDtypeStruct((rows, sl), F32),
        ),
        in_specs=[
            pl.BlockSpec((1, pos, width), lambda i: (i, 0, 0)),
            pl.BlockSpec((count, packed, 128), lambda i: (0, 0, 0)),
        ],
        out_specs=(
            pl.BlockSpec((1, pos, width), lambda i: (i, 0, 0)),
            pl.BlockSpec((rows, sl), fixed),
            pl.BlockSpec((rows, sl), fixed),
        ),
    )(grads, sums)
    return grads[None, :, None], first.T, second.T


def solution(mesh):
    n, nb = mesh.shape["seq"], mesh.shape["dp"]

    def chosen(*args):
        cot = args[2]
        _, frames, pos, width = cot.shape
        fits = frames == 1 and pos == 128 and width == HEADS * HD and n % 2 == 0 and nb % 2 == 0
        fits = fits and n > 2 and nb > 2 and HEADS % n == 0
        if fits and width // n % 16 == 0 and width // nb % 16 == 0:
            return kernel_body(n, nb, *args)
        return body(*args)

    return jax.shard_map(
        chosen,
        mesh=mesh,
        in_specs=(
            P("dp", None, "seq", None, None),
            P("dp", None, "seq", None, None),
            P("dp", "seq", None, None),
            P("dp", None),
            P("dp", None),
            P(),
            P("dp", None),
        ),
        out_specs=(P("dp", None, "seq", None, None), P("seq", "dp"), P("seq", "dp")),
        check_vma=False,
    )
```

```python
import functools

import jax
import jax.numpy as jnp
from jax import lax
from jax.experimental import pallas as pl
from jax.experimental.pallas import tpu as pltpu
from jax.sharding import PartitionSpec as P

HEADS = 16
HD = 72
MESH = pl.DeviceIdType.MESH
F32 = jnp.float32
BF16 = jnp.bfloat16


def attend(queries, key_block, value_block, key_keep, score_form, mix_form):
    head_split = queries.shape[:-1] + (HEADS, HD)
    q_heads = queries.reshape(head_split)
    k_heads = key_block.reshape(head_split)
    v_heads = value_block.reshape(head_split)
    scores = jnp.einsum(score_form, q_heads, k_heads, preferred_element_type=jnp.float32) * HD ** (
        -0.5
    )
    scores = jnp.where(key_keep[:, None, None, :], scores, -1e30)
    shifted = scores - jnp.max(scores, axis=-1, keepdims=True)
    expo = jnp.exp(shifted)
    attention_weights = (expo / jnp.sum(expo, axis=-1, keepdims=True)).astype(jnp.bfloat16)
    mixed = jnp.einsum(mix_form, attention_weights, v_heads, preferred_element_type=jnp.float32)
    return mixed.reshape(queries.shape)


def body(
    spatial_qkv, temporal_qkv, cotangent, spatial_gate, temporal_gate, temporal_proj, live_counts
):
    spatial = spatial_qkv[0]
    temporal = temporal_qkv[0]
    incoming = cotangent[0]
    frame_count, position_count, width = incoming.shape
    group_size = lax.axis_size("seq")
    member = lax.axis_index("seq")
    live_frames = live_counts[0, 0]
    live_positions = live_counts[0, 1]
    frame_ids = member * frame_count + jnp.arange(frame_count, dtype=jnp.int32)
    position_ids = jnp.arange(position_count, dtype=jnp.int32)
    token_mask = (
        (frame_ids[:, None] < live_frames) & (position_ids[None, :] < live_positions)
    ).astype(jnp.float32)
    flowing = token_mask[:, :, None] * incoming.astype(jnp.float32)
    temporal_error = (flowing * temporal_gate[0]).astype(jnp.bfloat16)
    temporal_back = lax.dot_general(
        temporal_error, temporal_proj, (((2,), (1,)), ((), ())), preferred_element_type=jnp.float32
    ).astype(jnp.bfloat16)
    stacked = jnp.concatenate([temporal, temporal_back[None]], axis=0)
    exchanged = lax.all_to_all(stacked, "seq", split_axis=2, concat_axis=1, tiled=True)
    spatial_keep = position_ids[None, :] < live_positions
    spatial_out = attend(
        spatial[0], spatial[1], spatial[2], spatial_keep, "bqhd,bkhd->bhqk", "bhqk,bkhd->bqhd"
    ).astype(jnp.bfloat16)
    total_frames = exchanged.shape[1]
    slice_positions = exchanged.shape[2]
    temporal_keep = jnp.broadcast_to(
        jnp.arange(total_frames, dtype=jnp.int32)[None, :] < live_frames,
        (slice_positions, total_frames),
    )

    def temporal_attend(queries, key_block, value_block):
        return attend(
            queries, key_block, value_block, temporal_keep, "qbhd,kbhd->bhqk", "bhqk,kbhd->qbhd"
        )

    temporal_result, pullback = jax.vjp(temporal_attend, exchanged[0], exchanged[1], exchanged[2])
    temporal_out = temporal_result.astype(jnp.bfloat16)
    input_grads = jnp.stack(pullback(exchanged[3].astype(jnp.float32)))
    temporal_frames = lax.all_to_all(temporal_out, "seq", split_axis=0, concat_axis=1, tiled=True)
    grads_home = lax.all_to_all(input_grads, "seq", split_axis=1, concat_axis=2, tiled=True)
    tokens = frame_count * position_count
    flat_spatial = spatial_out.reshape(tokens, width)
    flat_temporal = temporal_frames.reshape(tokens, width)
    slice_width = width // group_size
    column_spatial, column_temporal = (
        lax.all_to_all(flat_spatial, "seq", split_axis=1, concat_axis=0, tiled=True),
        lax.all_to_all(flat_temporal, "seq", split_axis=1, concat_axis=0, tiled=True),
    )
    spatial_scale = spatial_gate[0]
    temporal_scale = temporal_gate[0]
    starting = jnp.zeros((slice_width, 2, width), jnp.float32)
    cot_piece = lax.all_gather(incoming.reshape(tokens, width), "seq", axis=0, tiled=True)
    shards = cot_piece.shape[0] // tokens

    def one_block(block, total):
        offset = (block * tokens).astype(jnp.int32)
        rows = lax.dynamic_slice_in_dim(cot_piece, offset, tokens, 0)
        token_index = offset + jnp.arange(tokens, dtype=jnp.int32)
        frame_of = token_index // position_count
        position_of = token_index % position_count
        row_keep = ((frame_of < live_frames) & (position_of < live_positions)).astype(jnp.float32)
        masked_rows = row_keep[:, None] * rows.astype(jnp.float32)
        error_first = (masked_rows * spatial_scale).astype(jnp.bfloat16)
        error_second = (masked_rows * temporal_scale).astype(jnp.bfloat16)
        cols_first = lax.dynamic_slice_in_dim(column_spatial, offset, tokens, 0)
        cols_second = lax.dynamic_slice_in_dim(column_temporal, offset, tokens, 0)
        part_first = lax.dot_general(
            cols_first, error_first, (((0,), (0,)), ((), ())), preferred_element_type=jnp.float32
        )
        part_second = lax.dot_general(
            cols_second, error_second, (((0,), (0,)), ((), ())), preferred_element_type=jnp.float32
        )
        part_first = part_first.astype(jnp.bfloat16).astype(jnp.float32)
        part_second = part_second.astype(jnp.bfloat16).astype(jnp.float32)
        return total + jnp.stack([part_first, part_second], axis=1)

    partial_sum = lax.fori_loop(0, shards, one_block, starting)
    summed = lax.psum_scatter(partial_sum, "dp", scatter_dimension=2, tiled=True)
    return (grads_home[None], summed[:, 0], summed[:, 1])


def kernel(
    n, nb, units, counts, sgate, tgate, sqkv_hbm, tqkv_hbm, cot_hbm, proj_hbm,
    g_out, sum_out,
    sqkv, tqkv, cot, proj, cot_t, q_t, v_t, o_t, so, so_r, tq, tq_r, tqf, gf,
    err, err2, ot, do_t, part, xr, zs, zr, gs, gr,
    loc_sem, cs, cr, fs, fr, ss, sr, ts, tr, us, ur, xss, xrs, zss, zrs,
):
    me = lax.axis_index("seq")
    dp = lax.axis_index("dp")
    pos, width = cot.shape
    sl = width // n
    rows = width // nb
    pieces = tq.shape[1]
    half = sl // pieces
    ny, outer = n // 2, nb // 2
    y, c = me // 2, me % 2
    mate = y * 2 + 1 - c
    oz, ox = dp // 2, dp % 2
    scale = HD ** (-0.5)

    loads = [
        pltpu.make_async_copy(cot_hbm, cot, loc_sem.at[0]),
        pltpu.make_async_copy(sqkv_hbm, sqkv, loc_sem.at[1]),
        pltpu.make_async_copy(tqkv_hbm, tqkv, loc_sem.at[2]),
        pltpu.make_async_copy(proj_hbm.at[me], proj, loc_sem.at[3]),
    ]
    for load in loads:
        load.start()
    barrier = pltpu.get_barrier_semaphore()
    for j in range(1, n):
        pl.semaphore_signal(barrier, inc=1, device_id=(dp, (me + j) % n), device_id_type=MESH)
    pl.semaphore_signal(barrier, inc=1, device_id=(oz * 2 + 1 - ox, me), device_id_type=MESH)
    for j in range(1, outer):
        pl.semaphore_signal(
            barrier, inc=1, device_id=((oz + j) % outer * 2 + ox, me), device_id_type=MESH
        )

    def remote(src, dst, s_sem, r_sem, to):
        return pltpu.make_async_remote_copy(
            src_ref=src, dst_ref=dst, send_sem=s_sem, recv_sem=r_sem, device_id=to,
            device_id_type=MESH,
        )

    def turned(value):
        return value.astype(F32).T

    loads[0].wait()
    cot_t[me] = turned(cot[...]).astype(BF16)
    pl.semaphore_wait(barrier, (n - 1) + 1 + (outer - 1))

    sent = []

    def send(copy):
        copy.start()
        sent.append(copy)

    def y_copy(j):
        return remote(
            cot_t.at[me], cot_t.at[me], cs.at[j - 1], cr.at[j - 1], (dp, (y + j) % ny * 2 + c)
        )

    def pass_copy(j, core):
        slot = (y + ny - j) % ny * 2 + core
        return remote(cot_t.at[slot], cot_t.at[slot], fs.at[j], fr.at[j], (dp, mate))

    for j in range(1, ny):
        send(y_copy(j))
    send(pass_copy(0, c))

    live_frames = counts[0, 0]
    live_positions = counts[0, 1]

    loads[1].wait()
    q_t[...] = turned(sqkv[0])
    v_t[...] = turned(sqkv[2])
    key_keep = lax.broadcasted_iota(jnp.int32, (pos, pos), 0) < live_positions
    for h in range(HEADS):
        low = h * HD
        w0 = low // 128 * 128
        w1 = -(-(low + HD) // 128) * 128
        row = lax.broadcasted_iota(jnp.int32, (w1 - w0, pos), 0)
        inside = (row >= low - w0) & (row < low - w0 + HD)
        q_win = jnp.where(inside, q_t[w0:w1, :], 0.0).astype(BF16)
        scores = jnp.dot(sqkv[1, :, w0:w1], q_win, preferred_element_type=F32) * scale
        scores = jnp.where(key_keep, scores, -1e30)
        expo = jnp.exp(scores - jnp.max(scores, axis=0, keepdims=True))
        weights = (expo / jnp.sum(expo, axis=0, keepdims=True)).astype(BF16)
        o_t[low : low + HD, :] = jnp.dot(
            v_t[low : low + HD, :].astype(BF16), weights, preferred_element_type=F32
        )
    for s in range(n):
        so[s, 0] = o_t[s * sl : (s + 1) * sl, :].astype(BF16)
    so_r[me] = so[me]

    def swap(src, dst, s_sem, r_sem, i=0):
        for j in range(1, n):
            to = (me + j) % n
            send(
                remote(
                    src.at[to, i], dst.at[me, i], s_sem.at[i, j - 1], r_sem.at[i, j - 1], (dp, to)
                )
            )

    def arrive(src, dst, s_sem, r_sem, i=0):
        for j in range(1, n):
            origin = (me + n - j) % n
            remote(
                src.at[origin, i], dst.at[origin, i], s_sem.at[i, j - 1], r_sem.at[i, j - 1],
                (dp, origin),
            ).wait_recv()

    swap(so, so_r, ss, sr)

    loads[2].wait()
    for m in range(3):
        flat = turned(tqkv[m]).astype(BF16)
        for s in range(n):
            for i in range(pieces):
                low = s * sl + i * half
                tq[s, i, m] = flat[low : low + half, :]
    tq_r[me] = tq[me]
    for i in range(pieces):
        swap(tq, tq_r, ts, tr, i)

    def gate_rows(gate):
        return jnp.broadcast_to(gate[...], (pos, width)).T

    for j in range(1, ny):
        slot = (y + ny - j) % ny * 2 + c
        remote(
            cot_t.at[slot], cot_t.at[slot], cs.at[j - 1], cr.at[j - 1], (dp, mate)
        ).wait_recv()
        send(pass_copy(j, c))
    for j in range(ny):
        pass_copy(j, 1 - c).wait_recv()

    lane = lax.broadcasted_iota(jnp.int32, (1, pos), 1)
    keep = [
        ((lane < live_positions) & (f < live_frames)).astype(F32) for f in range(n)
    ]

    def errors(target, gate):
        columns = gate_rows(gate)
        for f in range(n):
            target[:, f * pos : (f + 1) * pos] = (
                keep[f] * cot_t[f].astype(F32) * columns
            ).astype(BF16)

    order = list(range(1, outer)) + [0]

    def times(left, right):
        return lax.dot_general(left, right, (((1,), (1,)), ((), ())), preferred_element_type=F32)

    def product(p, source, outs):
        main, tail, groups, _ = units[p]
        if tail:
            short = rows // groups
            edges = []
            for k in range(groups):
                blank = [
                    jnp.zeros((size, outs.shape[1]), BF16)
                    for size in (k * tail, 128 - (k + 1) * tail)
                ]
                parts = [blank[0], outs[main:, :], blank[1]]
                edges.append(jnp.concatenate([v for v in parts if v.shape[0]], axis=0))
        for x in (1 - ox, ox):
            for j in order:
                d = (oz + j) % outer * 2 + x
                first = pl.multiple_of(d * rows, 16)
                wide = times(source[pl.ds(first, rows), :], outs[:main, :]).astype(BF16)
                for k in range(main // 128):
                    part[p, d, k * rows : (k + 1) * rows, :] = wide[:, k * 128 : (k + 1) * 128]
                if tail:
                    edge = functools.reduce(
                        jnp.add,
                        [
                            times(
                                source[pl.ds(pl.multiple_of(first + k * short, 16), short), :],
                                edges[k],
                            )
                            for k in range(groups)
                        ],
                    )
                    part[p, d, main // 128 * rows : units[p][3], :] = edge.astype(BF16)
                if x is not ox:
                    send(pair_copy(p, j))

    def pair_copy(p, j):
        z = (oz + j) % outer
        return remote(
            part.at[p, z * 2 + 1 - ox, : units[p][3]], xr.at[p, j, : units[p][3]], xss.at[p, j], xrs.at[p, j],
            (oz * 2 + 1 - ox, me),
        )

    def line_copy(p, j):
        z = (oz + j) % outer
        return remote(
            zs.at[p, j - 1, : units[p][3]], zr.at[p, j - 1, : units[p][3]],
            zss.at[p, j - 1], zrs.at[p, j - 1], (z * 2 + ox, me)
        )

    def line_start(p):
        for j in order:
            z = (oz + j) % outer
            pair_copy(p, j).wait_recv()
            if j:
                size = units[p][3]
                zs[p, j - 1, :size, :] = (
                    part[p, z * 2 + ox, :size, :].astype(F32) + xr[p, j, :size, :].astype(F32)
                ).astype(BF16)
                send(line_copy(p, j))

    def line_end(p):
        size = units[p][3]
        total = part[p, oz * 2 + ox, :size, :].astype(F32) + xr[p, 0, :size, :].astype(F32)
        for j in range(1, outer):
            line_copy(p, j).wait_recv()
            total = total + zr[p, j - 1, :size, :].astype(F32)
        sum_out[p, :size, :] = total

    errors(err, sgate)
    arrive(so, so_r, ss, sr)
    product(0, err, jnp.concatenate([so_r[f, 0] for f in range(n)], axis=1))

    errors(err2, tgate)
    loads[3].wait()
    do_t[...] = (
        jnp.dot(proj[...], err2[...], preferred_element_type=F32).astype(BF16).astype(F32)
    )
    heads = half // HD

    def forward(i):
        kept = []
        for f in range(n):
            for m in range(3):
                tqf[f, i, m] = tq_r[f, i, m].astype(F32)
        for h in range(heads):
            band = slice(h * HD, (h + 1) * HD)
            place = slice(i * half + h * HD, i * half + (h + 1) * HD)
            ks = [tqf[g, i, 1, band, :] for g in range(n)]
            vs = [tqf[g, i, 2, band, :] for g in range(n)]
            for f in range(n):
                q = tqf[f, i, 0, band, :]
                row = [
                    jnp.where(
                        g < live_frames, jnp.sum(q * ks[g], axis=0, keepdims=True) * scale, -1e30
                    )
                    for g in range(n)
                ]
                top = functools.reduce(jnp.maximum, row)
                expo = [jnp.exp(value - top) for value in row]
                total = functools.reduce(jnp.add, expo)
                soft = [value / total for value in expo]
                rounded = [value.astype(BF16).astype(F32) for value in soft]
                kept.append((soft, rounded))
                ot[place, f * pos : (f + 1) * pos] = functools.reduce(
                    jnp.add, [rounded[g] * vs[g] for g in range(n)]
                )
        return kept

    def backward(i, kept):
        for h in range(heads):
            band = slice(h * HD, (h + 1) * HD)
            place = slice(i * half + h * HD, i * half + (h + 1) * HD)
            backs = [do_t[place, f * pos : (f + 1) * pos] for f in range(n)]
            slopes = []
            for f in range(n):
                soft, _ = kept[h * n + f]
                dw = [
                    jnp.sum(backs[f] * tqf[g, i, 2, band, :], axis=0, keepdims=True)
                    .astype(BF16)
                    .astype(F32)
                    for g in range(n)
                ]
                mean = functools.reduce(jnp.add, [soft[g] * dw[g] for g in range(n)])
                slopes.append([soft[g] * (dw[g] - mean) * scale for g in range(n)])
            for f in range(n):
                gf[f, i, 0, band, :] = functools.reduce(
                    jnp.add, [slopes[f][g] * tqf[g, i, 1, band, :] for g in range(n)]
                )
                gf[f, i, 1, band, :] = functools.reduce(
                    jnp.add, [slopes[g][f] * tqf[g, i, 0, band, :] for g in range(n)]
                )
                gf[f, i, 2, band, :] = functools.reduce(
                    jnp.add, [kept[h * n + g][1][f] * backs[g] for g in range(n)]
                )
        for f in range(n):
            for m in range(3):
                gs[f, i, m] = gf[f, i, m].astype(BF16)
        swap(gs, gr, us, ur, i)

    for i in range(pieces):
        arrive(tq, tq_r, ts, tr, i)
        kept = forward(i)
        product(1 + i, err2, ot[i * half : (i + 1) * half, :].astype(BF16))
        backward(i, kept)
        if i == 0:
            line_start(0)
    gr[me] = gs[me]

    line_end(0)
    for i in range(pieces):
        line_start(1 + i)
    for i in range(pieces):
        arrive(gs, gr, us, ur, i)
    for m in range(3):
        for s in range(n):
            for i in range(pieces):
                low = s * sl + i * half
                q_t[low : low + half, :] = gr[s, i, m].astype(F32)
        g_out[m] = q_t[...].T.astype(BF16)
    for i in range(pieces):
        line_end(1 + i)
    for copy in sent:
        copy.wait_send()


def finish(units, grads, sums, g_out, sp_out, tp_out):
    g_out[...] = grads[...]
    rows = sp_out.shape[0]

    @pl.when(pl.program_id(0) == 0)
    def _():
        left = 0
        for p, (main, tail, groups, size) in enumerate(units):
            out = tp_out if p else sp_out
            for k in range(main // 128):
                low = left + k * 128
                out[:, low : low + 128] = sums[p, k * rows : (k + 1) * rows, :]
            if tail:
                short = rows // groups
                edge = sums[p, main // 128 * rows : size, :]
                low = left + main
                for k in range(groups):
                    out[k * short : (k + 1) * short, low : low + tail] = edge[
                        :, k * tail : (k + 1) * tail
                    ]
            left = left + main + tail if p else 0


def unit_of(columns, rows):
    main, tail = columns // 128 * 128, columns % 128
    groups = 1
    if tail:
        groups = max(g for g in range(1, 128 // tail + 1) if rows % (16 * g) == 0)
    return main, tail, groups, main // 128 * rows + (rows // groups if tail else 0)


def kernel_body(
    n, nb, spatial_qkv, temporal_qkv, cotangent, spatial_gate, temporal_gate, temporal_proj, live_counts
):
    pos, width = cotangent.shape[2:]
    sl, rows, outer, ny = width // n, width // nb, nb // 2, n // 2
    vm, dma = pltpu.VMEM, pltpu.SemaphoreType.DMA
    whole = pl.BlockSpec(memory_space=pltpu.VMEM)
    left = pl.BlockSpec(memory_space=pl.ANY)
    pieces = 2 if sl // HD % 2 == 0 and sl // 2 % 16 == 0 else 1
    half = sl // pieces
    units = [unit_of(sl, rows)] + [unit_of(half, rows)] * pieces
    count, packed = len(units), max(unit[3] for unit in units)
    grads, sums = pl.pallas_call(
        functools.partial(kernel, n, nb, units),
        out_shape=(
            jax.ShapeDtypeStruct((3, pos, width), BF16),
            jax.ShapeDtypeStruct((count, packed, 128), F32),
        ),
        in_specs=[pl.BlockSpec(memory_space=pltpu.SMEM), whole, whole, left, left, left, left],
        out_specs=(whole, whole),
        scratch_shapes=[
            vm((3, pos, width), BF16), vm((3, pos, width), BF16), vm((pos, width), BF16),
            vm((sl, width), BF16), vm((n, width, pos), BF16),
            vm((width, pos), F32), vm((width, pos), F32), vm((width, pos), F32),
            vm((n, 1, sl, pos), BF16), vm((n, 1, sl, pos), BF16),
            vm((n, pieces, 3, half, pos), BF16), vm((n, pieces, 3, half, pos), BF16),
            vm((n, pieces, 3, half, pos), F32), vm((n, pieces, 3, half, pos), F32),
            vm((width, n * pos), BF16), vm((width, n * pos), BF16),
            vm((sl, n * pos), F32), vm((sl, n * pos), F32),
            vm((count, nb, packed, 128), BF16), vm((count, outer, packed, 128), BF16),
            vm((count, outer - 1, packed, 128), BF16), vm((count, outer - 1, packed, 128), BF16),
            vm((n, pieces, 3, half, pos), BF16), vm((n, pieces, 3, half, pos), BF16),
            dma((4,)), dma((ny - 1,)), dma((ny - 1,)), dma((ny,)), dma((ny,)),
            dma((1, n - 1)), dma((1, n - 1)), dma((pieces, n - 1)), dma((pieces, n - 1)),
            dma((pieces, n - 1)), dma((pieces, n - 1)),
            dma((count, outer)), dma((count, outer)), dma((count, outer - 1)), dma((count, outer - 1)),
        ],
        compiler_params=pltpu.CompilerParams(
            collective_id=0, has_side_effects=True, vmem_limit_bytes=56 * 1024 * 1024
        ),
    )(
        live_counts, spatial_gate, temporal_gate,
        spatial_qkv.reshape(3, pos, width), temporal_qkv.reshape(3, pos, width),
        cotangent.reshape(pos, width), temporal_proj.reshape(n, sl, width),
    )
    fixed = lambda i: (0, 0)
    grads, first, second = pl.pallas_call(
        functools.partial(finish, units),
        grid=(1,),
        out_shape=(
            jax.ShapeDtypeStruct((3, pos, width), BF16),
            jax.ShapeDtypeStruct((rows, sl), F32),
            jax.ShapeDtypeStruct((rows, sl), F32),
        ),
        in_specs=[
            pl.BlockSpec((3, pos, width), lambda i: (0, 0, 0)),
            pl.BlockSpec((count, packed, 128), lambda i: (0, 0, 0)),
        ],
        out_specs=(
            pl.BlockSpec((3, pos, width), lambda i: (0, 0, 0)),
            pl.BlockSpec((rows, sl), fixed),
            pl.BlockSpec((rows, sl), fixed),
        ),
    )(grads, sums)
    return grads[None, :, None], first.T, second.T


def solution(mesh):
    n, nb = mesh.shape["seq"], mesh.shape["dp"]

    def chosen(*args):
        cot = args[2]
        _, frames, pos, width = cot.shape
        fits = frames == 1 and pos == 128 and width == HEADS * HD and n % 2 == 0 and nb % 2 == 0
        fits = fits and n > 2 and nb > 2 and HEADS % n == 0
        if fits and width // n % 16 == 0 and width // nb % 16 == 0:
            return kernel_body(n, nb, *args)
        return body(*args)

    return jax.shard_map(
        chosen,
        mesh=mesh,
        in_specs=(
            P("dp", None, "seq", None, None),
            P("dp", None, "seq", None, None),
            P("dp", "seq", None, None),
            P("dp", None),
            P("dp", None),
            P(),
            P("dp", None),
        ),
        out_specs=(P("dp", None, "seq", None, None), P("seq", "dp"), P("seq", "dp")),
        check_vma=False,
    )
```
